32 devices in a mesh: grp: 2 (over x), stretch: 4 (over y, core), head: 4 (over z).
Axes of the slice: x: 2, y: 2, z: 4, core: 2. Of those that a mesh axis runs over, the one named last changes fastest.
Arguments:
- queries: bfloat16 [2560, 3072], P(('grp', 'stretch'), 'head'), parts along dimension 0, may hold values from -6 to 6
- keys: bfloat16 [2560, 3072], P(('grp', 'stretch'), 'head'), parts along dimension 0, may hold values from -6 to 6
- values: bfloat16 [2560, 3072], P(('grp', 'stretch'), 'head'), parts along dimension 0, may hold values from -6 to 6
- out_grad: bfloat16 [2560, 3072], P(('grp', 'stretch', 'head')), parts along dimension 0, may hold values from -6 to 6
- reads: int32 [8, 4], P('grp'), parts along dimension 0, may hold values 0 or 1
- slot_block: int32 [8], P('grp'), parts along dimension 0, may hold values from 0 to 3, each once
Outputs:
- query_grad: bfloat16 [2560, 3072], P(('grp', 'stretch'), 'head'), parts along dimension 0
- key_grad: bfloat16 [2560, 3072], P(('grp', 'stretch'), 'head'), parts along dimension 0
- value_grad: bfloat16 [2560, 3072], P(('grp', 'stretch'), 'head'), parts along dimension 0
The draws below stay inside these ranges and needn't reach their ends.
There are 2 independent parts, one for each index of `grp`. The reference program is written for one: setup_inputs(seed, part) draws one part's arguments, and reference() takes and returns one part's arrays. A program takes and returns all parts, laid end to end along the dimension named above; each array names one. Nothing has to cross between parts.
Inputs may be any that keep to these rules, and one draw needn't show every extreme that they name: Only entries reads[a, b] with b < a are used; every block attends to itself. `slot_block`: A permutation of the 4 latent blocks.
All inputs are finite; a program needn't handle non-finite values.
Results may differ from the reference program's by a relative error of at most 0.038.
Values may be sent and summed in bfloat16 or wider, within the bound.
No kernel may reach another device: no remote copies, remote signals or barrier semaphores. Data moves between devices by JAX's collectives and lax.ppermute only.
A program may use at most 64 MiB of HBM per device.

```python
import math
import jax
import jax.numpy as jnp
from jax import lax

HEADS = 24
HD = 128
BLOCK_TOK = 320
BLOCKS = 4
TOKENS = 1280
FEAT = 3072


def pair_fields(key):
    base_q = jnp.clip(jax.random.normal(jax.random.fold_in(key, 201), (TOKENS, FEAT), jnp.float32), -4.0, 4.0)
    base_k = jnp.clip(jax.random.normal(jax.random.fold_in(key, 202), (TOKENS, FEAT), jnp.float32), -4.0, 4.0)
    return (base_q, base_k)


def draw_queries(key, part):
    return pair_fields(key)[0].astype(jnp.bfloat16)


def draw_keys(key, part):
    return pair_fields(key)[1].astype(jnp.bfloat16)


def place_ends(entries, stream_key, smallest, high):
    dims = entries.shape
    place = [jax.random.randint(jax.random.fold_in(stream_key, axis), (), 0, dims[axis]) for axis in range(len(dims))]
    entries = entries.at[tuple(place)].set(smallest)
    longest = dims.index(max(dims))
    place[longest] = (place[longest] + 1) % dims[longest]
    return entries.at[tuple(place)].set(high)


def steps_of(stream_key, shape, cuts, low, high):
    level, own = 1.0, jax.random.fold_in(stream_key, 6)
    for position, parts in cuts:
        steps = jnp.exp(jax.random.uniform(jax.random.fold_in(own, position), (parts,), jnp.float32, low / len(cuts), high / len(cuts)))
        level = level * jnp.repeat(steps, shape[position] // parts).reshape([-1 if axis == position else 1 for axis in range(len(shape))])
    return level


def noise(own_key, dims, scale, bound, shards=(), dtype=jnp.bfloat16):
    loudness = steps_of(own_key, dims, shards, -0.22, 0.18) if shards else 1.0
    array = jax.random.normal(own_key, dims, jnp.float32) * scale * loudness
    return jnp.minimum(jnp.maximum(array, -bound), bound).astype(dtype)


def setup_inputs(seed: int = 0, part: int = 0) -> dict:
    key_of = jax.random.split(jax.random.key(seed), 7)
    part_keys = jax.random.split(jax.random.fold_in(key_of[6], part), 7)
    queries = draw_queries(jax.random.fold_in(jax.random.fold_in(key_of[6], part), 71), part)
    keys = draw_keys(jax.random.fold_in(jax.random.fold_in(key_of[6], part), 71), part)
    values = noise(part_keys[2], (TOKENS, FEAT), 1.0, 6.0, ((0, 4), (1, 4)))
    out_grad = noise(part_keys[3], (TOKENS, FEAT), 1.0, 6.0, ((0, 16),))
    reads = place_ends((jax.random.randint(part_keys[4], (BLOCKS, BLOCKS), 0, 4) < 3).astype(jnp.int32), jax.random.fold_in(part_keys[4], 1), 0, 1)
    slot_block = jax.random.permutation(part_keys[5], BLOCKS).astype(jnp.int32)
    return dict(queries=queries, keys=keys, values=values, out_grad=out_grad, reads=reads, slot_block=slot_block)


def low(value):
    return lax.optimization_barrier(value.astype(jnp.bfloat16)).astype(jnp.float32)

def reference(queries, keys, values, out_grad, reads, slot_block):
    scale = 1.0 / math.sqrt(HD)
    q_all = queries.astype(jnp.float32).reshape(BLOCKS, BLOCK_TOK, HEADS, HD)
    g_all = out_grad.astype(jnp.float32).reshape(BLOCKS, BLOCK_TOK, HEADS, HD)
    key_full = keys.astype(jnp.float32).reshape(TOKENS, HEADS, HD)
    val_full = values.astype(jnp.float32).reshape(TOKENS, HEADS, HD)
    first = slot_block[:, None]
    second = slot_block[None, :]
    linked = reads[first, second]
    open_pairs = (first == second) | (second < first) & (linked == 1)
    key_masks = jnp.repeat(open_pairs, BLOCK_TOK, axis=1)

    def step(carry, block):
        key_acc, val_acc = carry
        q_rows, g_rows, mask = block
        logits = jnp.einsum('qhd,khd->hqk', q_rows, key_full) * scale
        masked_logits = jnp.where(mask[None, None, :], logits, -jnp.inf)
        top = lax.optimization_barrier(jnp.max(masked_logits, axis=-1, keepdims=True))
        lse = top + jnp.log(lax.optimization_barrier(jnp.sum(jnp.exp(masked_logits - top), axis=-1, keepdims=True)))
        prob = jnp.where(mask[None, None, :], jnp.exp(logits - lse), jnp.float32(0.0))
        prob_low = low(prob)
        attended = low(jnp.einsum('hqk,khd->qhd', prob_low, val_full))
        delta = lax.optimization_barrier(jnp.sum(g_rows * attended, axis=-1)).T
        dprob = jnp.einsum('qhd,khd->hqk', g_rows, val_full)
        dlogit = low(prob * (dprob - delta[:, :, None]) * scale)
        dquery = jnp.einsum('hqk,khd->qhd', dlogit, key_full).astype(jnp.bfloat16)
        key_part = low(jnp.einsum('hqk,qhd->khd', dlogit, q_rows))
        val_part = low(jnp.einsum('hqk,qhd->khd', prob_low, g_rows))
        return ((key_acc + key_part, val_acc + val_part), dquery)
    zeros = jnp.zeros((TOKENS, HEADS, HD), jnp.float32)
    (key_acc, val_acc), dquery = lax.scan(step, (zeros, zeros), (q_all, g_all, key_masks))
    query_grad = dquery.reshape(TOKENS, FEAT)
    key_grad = key_acc.reshape(TOKENS, FEAT).astype(jnp.bfloat16)
    value_grad = val_acc.reshape(TOKENS, FEAT).astype(jnp.bfloat16)
    return (query_grad, key_grad, value_grad)
```

```python
import functools
import math

import jax
import jax.numpy as jnp
from jax import lax
from jax.experimental import pallas as pl
from jax.experimental.pallas import tpu as pltpu
from jax.sharding import PartitionSpec as P

HD = 128
LOG2E = 1.4426950408889634
CLOSED = -1e30


def pick_rows(table, visit_sequence, index):
    return jnp.sum(jnp.where((visit_sequence == index)[:, None], table, 0), axis=0)


def slopes(q_rows, g_rows, row_logsumexp, row_delta, key_rows, val_rows, mask, scale):
    logits = (
        jnp.einsum("qhd,khd->hqk", q_rows, key_rows, preferred_element_type=jnp.float32) * scale
    )
    prob = jnp.where(mask, jnp.exp(logits - row_logsumexp[:, :, None]), jnp.float32(0.0))
    dprob = jnp.einsum("qhd,khd->hqk", g_rows, val_rows, preferred_element_type=jnp.float32)
    dlogit = (prob * (dprob - row_delta[:, :, None]) * scale).astype(jnp.bfloat16)
    return (prob.astype(jnp.bfloat16), dlogit)


def gathered(queries, keys, values, out_grad, reads, slot_block):
    rows, width = queries.shape
    heads = width // HD
    scale = 1.0 / math.sqrt(HD)
    grads_in = lax.all_to_all(out_grad, "head", split_axis=1, concat_axis=0, tiled=True)
    slot_count = lax.axis_size("stretch")
    slot = lax.axis_index("stretch")
    visit_sequence = jnp.arange(slot_count, dtype=jnp.int32)
    mine = jnp.sum(jnp.where(visit_sequence == slot, slot_block, 0))
    same_table = slot_block[:, None] == visit_sequence[None, :]
    read_row = pick_rows(reads, visit_sequence, mine)
    own_reads = jnp.sum(jnp.where(same_table, read_row[None, :], 0), axis=1)
    key_open = (slot_block == mine) | (slot_block < mine) & (own_reads == 1)
    q_three = queries.reshape(rows, heads, HD)
    g_three = grads_in.reshape(rows, heads, HD)
    key_whole, val_whole = (
        lax.all_gather(keys, "stretch", axis=0, tiled=True),
        lax.all_gather(values, "stretch", axis=0, tiled=True),
    )
    total = key_whole.shape[0]
    per_iteration = -(-512 // rows)
    while slot_count % per_iteration:
        per_iteration -= 1
    span = rows * per_iteration
    nspan = total // span
    key_mask = jnp.repeat(key_open, rows)
    key_blocks = key_whole.reshape(nspan, span, heads, HD)
    val_blocks = val_whole.reshape(nspan, span, heads, HD)
    mask_blocks = key_mask.reshape(nspan, span)

    def forward_step(carry, block):
        top, mass, accum = carry
        key_block_tile, value_block_tile, open_blk = block
        logits = (
            jnp.einsum("qhd,khd->hqk", q_three, key_block_tile, preferred_element_type=jnp.float32)
            * scale
        )
        masked_logits = jnp.where(open_blk[None, None, :], logits, jnp.float32(-1e30))
        new_top = jnp.maximum(top, jnp.max(masked_logits, axis=-1))
        weights = jnp.where(
            open_blk[None, None, :], jnp.exp(masked_logits - new_top[:, :, None]), jnp.float32(0.0)
        )
        shrink = jnp.exp(top - new_top)
        mass = mass * shrink + jnp.sum(weights, axis=-1)
        accum = accum * shrink[:, :, None] + jnp.einsum(
            "hqk,khd->hqd",
            weights.astype(jnp.bfloat16),
            value_block_tile,
            preferred_element_type=jnp.float32,
        )
        return ((new_top, mass, accum), None)

    start_top = jnp.full((heads, rows), -1e30, jnp.float32)
    start_mass = jnp.zeros((heads, rows), jnp.float32)
    start_accum = jnp.zeros((heads, rows, HD), jnp.float32)
    (top, mass, accum), _ = lax.scan(
        forward_step, (start_top, start_mass, start_accum), (key_blocks, val_blocks, mask_blocks)
    )
    row_logsumexp = top + jnp.log(mass)
    attended = (accum / mass[:, :, None]).astype(jnp.bfloat16)
    row_delta = jnp.einsum("qhd,hqd->hq", g_three, attended, preferred_element_type=jnp.float32)
    dquery_start = jnp.zeros((rows, heads, HD), jnp.float32)

    def joined_step(dquery, block):
        key_block_tile, value_block_tile, open_blk = block
        prob_low, dlogit = slopes(
            q_three,
            g_three,
            row_logsumexp,
            row_delta,
            key_block_tile,
            value_block_tile,
            open_blk[None, None, :],
            scale,
        )
        dquery = dquery + jnp.einsum(
            "hqk,khd->qhd", dlogit, key_block_tile, preferred_element_type=jnp.float32
        )
        dkey = jnp.einsum("hqk,qhd->khd", dlogit, q_three, preferred_element_type=jnp.float32)
        dval = jnp.einsum("hqk,qhd->khd", prob_low, g_three, preferred_element_type=jnp.float32)
        terms = jnp.concatenate([dkey.reshape(span, width), dval.reshape(span, width)], axis=1)
        return (dquery, terms)

    dquery, stacked = lax.scan(joined_step, dquery_start, (key_blocks, val_blocks, mask_blocks))
    query_grad = dquery.reshape(rows, width).astype(jnp.bfloat16)
    both = lax.psum_scatter(
        stacked.reshape(total, 2 * width).astype(jnp.bfloat16),
        "stretch",
        scatter_dimension=0,
        tiled=True,
    ).astype(jnp.float32)
    key_grad = both[:, :width].astype(jnp.bfloat16)
    value_grad = both[:, width:].astype(jnp.bfloat16)
    return (query_grad, key_grad, value_grad)


NT = (((1,), (1,)), ((), ()))
TN = (((0,), (0,)), ((), ()))


def head_kernel(
    pos_ref,
    block_ref,
    reads_ref,
    q_ref,
    k_ref,
    v_ref,
    ks_ref,
    vs_ref,
    rec_ref,
    recs_ref,
    g0_ref,
    g1_ref,
    g2_ref,
    g3_ref,
    dq_ref,
    keep_ref,
    send_ref,
    q_all,
    g_all,
    k_all,
    v_all,
    score,
    dprob,
    prob_low,
    dlog_low,
):
    rows = q_ref.shape[0]
    grad_rows = g0_ref.shape[1]
    slot, place = pos_ref[0], pos_ref[1]
    nh = rows // grad_rows
    scale = 1.0 / math.sqrt(HD)
    q_all[:rows] = q_ref[...]
    q_all[rows:] = rec_ref[:, :HD]
    k_all[:rows] = k_ref[...]
    k_all[rows : 2 * rows] = rec_ref[:, HD : 2 * HD]
    k_all[2 * rows : 3 * rows] = ks_ref[...]
    k_all[3 * rows :] = recs_ref[:, HD : 2 * HD]
    v_all[:rows] = v_ref[...]
    v_all[rows : 2 * rows] = rec_ref[:, 2 * HD :]
    v_all[2 * rows : 3 * rows] = vs_ref[...]
    v_all[3 * rows :] = recs_ref[:, 2 * HD :]
    for d, g_ref in enumerate((g0_ref, g1_ref, g2_ref, g3_ref)):
        base = lax.rem(place - d + nh, nh) * grad_rows
        for i in range(2):
            at = pl.multiple_of(base + i * rows, 16)
            g_all[pl.ds(at, grad_rows), :] = g_ref[i]

    q_slots = [slot, slot ^ 2]
    k_slots = [slot, slot ^ 2, slot ^ 1, slot ^ 3]
    lane = lax.broadcasted_iota(jnp.int32, (1, 2 * rows), 1)

    def shut(i, j):
        first, second = block_ref[q_slots[i]], block_ref[k_slots[j]]
        linked = reads_ref[first, second]
        seen = (first == second) | ((second < first) & (linked == 1))
        return jnp.where(seen, jnp.float32(0.0), jnp.float32(CLOSED))

    top = jnp.full((1, 2 * rows), CLOSED, jnp.float32)
    for j in range(4):
        at = slice(j * rows, (j + 1) * rows)
        s = lax.dot_general(k_all[at], q_all[...], NT, preferred_element_type=jnp.float32)
        s = s * (scale * LOG2E) + jnp.where(lane < rows, shut(0, j), shut(1, j))
        score[at] = s
        top = jnp.maximum(top, jnp.max(s, axis=0, keepdims=True))
    mass = jnp.zeros((1, 2 * rows), jnp.float32)
    mixed = jnp.zeros((1, 2 * rows), jnp.float32)
    for j in range(4):
        at = slice(j * rows, (j + 1) * rows)
        t = lax.dot_general(v_all[at], g_all[...], NT, preferred_element_type=jnp.float32)
        e = jnp.exp2(score[at] - top)
        score[at] = e
        dprob[at] = t
        mass = mass + jnp.sum(e, axis=0, keepdims=True)
        mixed = mixed + jnp.sum(e * t, axis=0, keepdims=True)
    inv = 1.0 / mass
    delta = mixed * inv
    inv_scaled = inv * scale
    dq = jnp.zeros((2 * rows, HD), jnp.float32)
    for j in range(4):
        at = slice(j * rows, (j + 1) * rows)
        e = score[at]
        prob_low[at] = (e * inv).astype(jnp.bfloat16)
        dlog_low[at] = ((e * inv_scaled) * (dprob[at] - delta)).astype(jnp.bfloat16)
        dk = jnp.dot(dlog_low[at], q_all[...], preferred_element_type=jnp.float32)
        dv = jnp.dot(prob_low[at], g_all[...], preferred_element_type=jnp.float32)
        dq = dq + lax.dot_general(
            dlog_low[at], k_all[at], TN, preferred_element_type=jnp.float32
        )
        if j < 2:
            keep_ref[j * rows : (j + 1) * rows, :HD] = dk
            keep_ref[j * rows : (j + 1) * rows, HD:] = dv
        else:
            send_ref[(j - 2) * rows : (j - 1) * rows, :HD] = dk.astype(jnp.bfloat16)
            send_ref[(j - 2) * rows : (j - 1) * rows, HD:] = dv.astype(jnp.bfloat16)
    dq_ref[...] = dq.astype(jnp.bfloat16)


def head_call(hh, index, pos, slot_block, reads, arrays, rec, recs, grads):
    rows = rec.shape[0]
    grad_rows = grads[0].shape[1]
    column = lambda g, p, b, r: (0, (p[0] // 2) * hh + index)
    whole = lambda g, p, b, r: (0, 0)
    own = pl.BlockSpec((rows, HD), column)
    seen = pl.BlockSpec((rows, 3 * HD), whole)
    grad = pl.BlockSpec((2, grad_rows, HD), lambda g, p, b, r: (0, 0, index))
    return pl.pallas_call(
        head_kernel,
        name="attend_head",
        out_shape=(
            jax.ShapeDtypeStruct((2 * rows, HD), jnp.bfloat16),
            jax.ShapeDtypeStruct((2 * rows, 2 * HD), jnp.float32),
            jax.ShapeDtypeStruct((2 * rows, 2 * HD), jnp.bfloat16),
        ),
        grid_spec=pltpu.PrefetchScalarGridSpec(
            num_scalar_prefetch=3,
            grid=(1,),
            in_specs=[own] * 5 + [seen] * 2 + [grad] * 4,
            out_specs=[
                pl.BlockSpec((2 * rows, HD), whole),
                pl.BlockSpec((2 * rows, 2 * HD), whole),
                pl.BlockSpec((2 * rows, 2 * HD), whole),
            ],
            scratch_shapes=[
                pltpu.VMEM((2 * rows, HD), jnp.bfloat16),
                pltpu.VMEM((2 * rows, HD), jnp.bfloat16),
                pltpu.VMEM((4 * rows, HD), jnp.bfloat16),
                pltpu.VMEM((4 * rows, HD), jnp.bfloat16),
                pltpu.VMEM((4 * rows, 2 * rows), jnp.float32),
                pltpu.VMEM((4 * rows, 2 * rows), jnp.float32),
                pltpu.VMEM((4 * rows, 2 * rows), jnp.bfloat16),
                pltpu.VMEM((4 * rows, 2 * rows), jnp.bfloat16),
            ],
        ),
        compiler_params=pltpu.CompilerParams(vmem_limit_bytes=32 << 20),
        cost_estimate=pl.CostEstimate(
            flops=5 * 2 * 8 * rows * rows * HD,
            transcendentals=8 * rows * rows,
            bytes_accessed=rows * HD * 2 * 30,
        ),
    )(pos, slot_block, reads, *arrays, rec, recs, *grads)


def merge_kernel(dq_ref, keep_ref, got_ref, stay_ref, back_ref):
    rows = stay_ref.shape[0]
    total = (keep_ref[...] + got_ref[...].astype(jnp.float32)).astype(jnp.bfloat16)
    stay_ref[:, :HD] = dq_ref[:rows]
    stay_ref[:, HD:] = total[:rows]
    back_ref[:, :HD] = dq_ref[rows:]
    back_ref[:, HD:] = total[rows:]


def merge_call(dq, keep, got):
    rows = dq.shape[0] // 2
    shape = jax.ShapeDtypeStruct((rows, 3 * HD), jnp.bfloat16)
    return pl.pallas_call(
        merge_kernel,
        name="merge_head",
        out_shape=(shape, shape),
        compiler_params=pltpu.CompilerParams(vmem_limit_bytes=8 << 20),
        cost_estimate=pl.CostEstimate(
            flops=rows * HD * 8, transcendentals=0, bytes_accessed=rows * HD * 40
        ),
    )(dq, keep, got)


def finish_kernel(hh, pos_ref, *refs):
    stay, back, outs = refs[:hh], refs[hh : 2 * hh], refs[2 * hh :]
    half = pos_ref[0] // 2
    for i in range(hh):
        near = pl.ds(pl.multiple_of((half * hh + i) * HD, HD), HD)
        far = pl.ds(pl.multiple_of(((1 - half) * hh + i) * HD, HD), HD)
        for t, out in enumerate(outs):
            out[:, near] = stay[i][:, t * HD : (t + 1) * HD]
            out[:, far] = back[i][:, t * HD : (t + 1) * HD]


def finish_call(pos, stay, back):
    hh = len(stay)
    rows = stay[0].shape[0]
    shape = jax.ShapeDtypeStruct((rows, 2 * hh * HD), jnp.bfloat16)
    vmem = pl.BlockSpec(memory_space=pltpu.VMEM)
    return pl.pallas_call(
        functools.partial(finish_kernel, hh),
        name="finish",
        out_shape=(shape, shape, shape),
        in_specs=[pl.BlockSpec(memory_space=pltpu.SMEM)] + [vmem] * (2 * hh),
        out_specs=[vmem] * 3,
        compiler_params=pltpu.CompilerParams(vmem_limit_bytes=12 << 20),
        cost_estimate=pl.CostEstimate(
            flops=0, transcendentals=0, bytes_accessed=rows * HD * hh * 24
        ),
    )(pos, *stay, *back)


def halved(queries, keys, values, out_grad, reads, slot_block):
    rows, width = queries.shape
    half = width // 2
    hh = half // HD
    grad_rows = out_grad.shape[0]
    nh = lax.axis_size("head")
    slot = lax.axis_index("stretch")
    place = lax.axis_index("head")
    side = slot // 2
    pos = jnp.stack([slot, place]).astype(jnp.int32)
    across = lambda x: lax.ppermute(x, "stretch", [(i, i ^ 2) for i in range(4)])
    beside = lambda x: lax.ppermute(x, "stretch", [(i, i ^ 1) for i in range(4)])

    g_four = out_grad.reshape(grad_rows, nh, 2, half)
    g_keep = lax.dynamic_index_in_dim(g_four, side, 2, keepdims=False)
    g_got = across(lax.dynamic_index_in_dim(g_four, 1 - side, 2, keepdims=False))

    def far_head(i):
        at = ((1 - side) * hh + i) * HD
        return jnp.concatenate(
            [lax.dynamic_slice_in_dim(x, at, HD, axis=1) for x in (queries, keys, values)], axis=1
        )

    rec = [across(far_head(i)) for i in range(hh)]
    k_side, v_side = beside(keys), beside(values)
    recs = [beside(x) for x in rec]

    grads = []
    for d in range(nh):
        target = lax.rem(place + d, nh)
        blk = jnp.stack(
            [lax.dynamic_index_in_dim(x, target, 1, keepdims=False) for x in (g_keep, g_got)]
        )
        if d:
            blk = lax.ppermute(blk, "head", [(i, (i + d) % nh) for i in range(nh)])
        grads.append(blk)

    arrays = (queries, keys, values, k_side, v_side)
    stay, back = [], []
    for i in range(hh):
        dq, keep, send = head_call(
            hh, i, pos, slot_block, reads, arrays, rec[i], recs[i], grads
        )
        near, far = merge_call(dq, keep, beside(send))
        stay.append(near)
        back.append(across(far))
    return finish_call(pos, stay, back)


def solution(mesh):
    def shards(queries, keys, values, out_grad, reads, slot_block):
        heads = queries.shape[1] // HD
        if mesh.shape["stretch"] == 4 and mesh.shape["head"] == 4 and heads % 2 == 0:
            return halved(queries, keys, values, out_grad, reads, slot_block)
        return gathered(queries, keys, values, out_grad, reads, slot_block)

    return jax.shard_map(
        shards,
        mesh=mesh,
        in_specs=(
            P(("grp", "stretch"), "head"),
            P(("grp", "stretch"), "head"),
            P(("grp", "stretch"), "head"),
            P(("grp", "stretch", "head"), None),
            P("grp", None),
            P("grp"),
        ),
        out_specs=(
            P(("grp", "stretch"), "head"),
            P(("grp", "stretch"), "head"),
            P(("grp", "stretch"), "head"),
        ),
        check_vma=False,
    )
```

```python
import functools
import math

import jax
import jax.numpy as jnp
from jax import lax
from jax.experimental import pallas as pl
from jax.experimental.pallas import tpu as pltpu
from jax.sharding import PartitionSpec as P

HD = 128
LOG2E = 1.4426950408889634
CLOSED = -1e30
SCALE = 1.0 / math.sqrt(HD)


def pick_rows(table, visit_sequence, index):
    return jnp.sum(jnp.where((visit_sequence == index)[:, None], table, 0), axis=0)


def slopes(q_rows, g_rows, row_logsumexp, row_delta, key_rows, val_rows, mask, scale):
    logits = (
        jnp.einsum("qhd,khd->hqk", q_rows, key_rows, preferred_element_type=jnp.float32) * scale
    )
    prob = jnp.where(mask, jnp.exp(logits - row_logsumexp[:, :, None]), jnp.float32(0.0))
    dprob = jnp.einsum("qhd,khd->hqk", g_rows, val_rows, preferred_element_type=jnp.float32)
    dlogit = (prob * (dprob - row_delta[:, :, None]) * scale).astype(jnp.bfloat16)
    return (prob.astype(jnp.bfloat16), dlogit)


def gathered(queries, keys, values, out_grad, reads, slot_block):
    rows, width = queries.shape
    heads = width // HD
    scale = 1.0 / math.sqrt(HD)
    grads_in = lax.all_to_all(out_grad, "head", split_axis=1, concat_axis=0, tiled=True)
    slot_count = lax.axis_size("stretch")
    slot = lax.axis_index("stretch")
    visit_sequence = jnp.arange(slot_count, dtype=jnp.int32)
    mine = jnp.sum(jnp.where(visit_sequence == slot, slot_block, 0))
    same_table = slot_block[:, None] == visit_sequence[None, :]
    read_row = pick_rows(reads, visit_sequence, mine)
    own_reads = jnp.sum(jnp.where(same_table, read_row[None, :], 0), axis=1)
    key_open = (slot_block == mine) | (slot_block < mine) & (own_reads == 1)
    q_three = queries.reshape(rows, heads, HD)
    g_three = grads_in.reshape(rows, heads, HD)
    key_whole, val_whole = (
        lax.all_gather(keys, "stretch", axis=0, tiled=True),
        lax.all_gather(values, "stretch", axis=0, tiled=True),
    )
    total = key_whole.shape[0]
    per_iteration = -(-512 // rows)
    while slot_count % per_iteration:
        per_iteration -= 1
    span = rows * per_iteration
    nspan = total // span
    key_mask = jnp.repeat(key_open, rows)
    key_blocks = key_whole.reshape(nspan, span, heads, HD)
    val_blocks = val_whole.reshape(nspan, span, heads, HD)
    mask_blocks = key_mask.reshape(nspan, span)

    def forward_step(carry, block):
        top, mass, accum = carry
        key_block_tile, value_block_tile, open_blk = block
        logits = (
            jnp.einsum("qhd,khd->hqk", q_three, key_block_tile, preferred_element_type=jnp.float32)
            * scale
        )
        masked_logits = jnp.where(open_blk[None, None, :], logits, jnp.float32(-1e30))
        new_top = jnp.maximum(top, jnp.max(masked_logits, axis=-1))
        weights = jnp.where(
            open_blk[None, None, :], jnp.exp(masked_logits - new_top[:, :, None]), jnp.float32(0.0)
        )
        shrink = jnp.exp(top - new_top)
        mass = mass * shrink + jnp.sum(weights, axis=-1)
        accum = accum * shrink[:, :, None] + jnp.einsum(
            "hqk,khd->hqd",
            weights.astype(jnp.bfloat16),
            value_block_tile,
            preferred_element_type=jnp.float32,
        )
        return ((new_top, mass, accum), None)

    start_top = jnp.full((heads, rows), -1e30, jnp.float32)
    start_mass = jnp.zeros((heads, rows), jnp.float32)
    start_accum = jnp.zeros((heads, rows, HD), jnp.float32)
    (top, mass, accum), _ = lax.scan(
        forward_step, (start_top, start_mass, start_accum), (key_blocks, val_blocks, mask_blocks)
    )
    row_logsumexp = top + jnp.log(mass)
    attended = (accum / mass[:, :, None]).astype(jnp.bfloat16)
    row_delta = jnp.einsum("qhd,hqd->hq", g_three, attended, preferred_element_type=jnp.float32)
    dquery_start = jnp.zeros((rows, heads, HD), jnp.float32)

    def joined_step(dquery, block):
        key_block_tile, value_block_tile, open_blk = block
        prob_low, dlogit = slopes(
            q_three,
            g_three,
            row_logsumexp,
            row_delta,
            key_block_tile,
            value_block_tile,
            open_blk[None, None, :],
            scale,
        )
        dquery = dquery + jnp.einsum(
            "hqk,khd->qhd", dlogit, key_block_tile, preferred_element_type=jnp.float32
        )
        dkey = jnp.einsum("hqk,qhd->khd", dlogit, q_three, preferred_element_type=jnp.float32)
        dval = jnp.einsum("hqk,qhd->khd", prob_low, g_three, preferred_element_type=jnp.float32)
        terms = jnp.concatenate([dkey.reshape(span, width), dval.reshape(span, width)], axis=1)
        return (dquery, terms)

    dquery, stacked = lax.scan(joined_step, dquery_start, (key_blocks, val_blocks, mask_blocks))
    query_grad = dquery.reshape(rows, width).astype(jnp.bfloat16)
    both = lax.psum_scatter(
        stacked.reshape(total, 2 * width).astype(jnp.bfloat16),
        "stretch",
        scatter_dimension=0,
        tiled=True,
    ).astype(jnp.float32)
    key_grad = both[:, :width].astype(jnp.bfloat16)
    value_grad = both[:, width:].astype(jnp.bfloat16)
    return (query_grad, key_grad, value_grad)


NT = (((1,), (1,)), ((), ()))
TN = (((0,), (0,)), ((), ()))


def prob_kernel(
    index,
    block_ref,
    reads_ref,
    q_ref,
    near_ref,
    side_ref,
    rec_ref,
    recs_ref,
    prob_ref,
    q_all,
    score,
):
    rows = q_ref.shape[0]
    own = slice(index * HD, (index + 1) * HD)
    slot = lax.axis_index("stretch")
    q_all[:rows] = q_ref[:, index * HD : (index + 1) * HD]
    q_all[rows:] = rec_ref[:, :HD]

    q_slots = [slot, slot ^ 2]
    k_slots = [slot, slot ^ 2, slot ^ 1, slot ^ 3]
    lane = lax.broadcasted_iota(jnp.int32, (1, 2 * rows), 1)

    def shut(i, j):
        first, second = block_ref[q_slots[i]], block_ref[k_slots[j]]
        linked = reads_ref[first, second]
        seen = (first == second) | ((second < first) & (linked == 1))
        return jnp.where(seen, jnp.float32(0.0), jnp.float32(CLOSED))

    pieces = (
        near_ref.at[:, own],
        rec_ref.at[:, HD : 2 * HD],
        side_ref.at[:, own],
        recs_ref.at[:, HD : 2 * HD],
    )
    top = jnp.full((1, 2 * rows), CLOSED, jnp.float32)
    for j, piece in enumerate(pieces):
        s = lax.dot_general(piece[...], q_all[...], NT, preferred_element_type=jnp.float32)
        s = s * (LOG2E / math.sqrt(HD)) + jnp.where(lane < rows, shut(0, j), shut(1, j))
        score[j * rows : (j + 1) * rows] = s
        top = jnp.maximum(top, jnp.max(s, axis=0, keepdims=True))
    mass = jnp.zeros((1, 2 * rows), jnp.float32)
    for j in range(4):
        at = slice(j * rows, (j + 1) * rows)
        e = jnp.exp2(score[at] - top)
        score[at] = e
        mass = mass + jnp.sum(e, axis=0, keepdims=True)
    inv = 1.0 / mass
    for j in range(4):
        at = slice(j * rows, (j + 1) * rows)
        prob_ref[at] = (score[at] * inv).astype(jnp.bfloat16)


def slope_kernel(
    hh,
    index,
    near_ref,
    side_ref,
    rec_ref,
    recs_ref,
    g0_ref,
    g1_ref,
    g2_ref,
    g3_ref,
    prob_ref,
    q_ref,
    dlog_ref,
    g_ref,
    send_ref,
    dprob,
):
    rows = rec_ref.shape[0]
    grad_rows = g0_ref.shape[1]
    place = lax.axis_index("head")
    nh = rows // grad_rows
    own = slice((hh + index) * HD, (hh + index + 1) * HD)
    for d, part_ref in enumerate((g0_ref, g1_ref, g2_ref, g3_ref)):
        base = lax.rem(place - d + nh, nh) * grad_rows
        for i in range(2):
            at = pl.multiple_of(base + i * rows, 16)
            g_ref[pl.ds(at, grad_rows), :] = part_ref[i, :, index * HD : (index + 1) * HD]
    pieces = (
        near_ref.at[:, own],
        rec_ref.at[:, 2 * HD :],
        side_ref.at[:, own],
        recs_ref.at[:, 2 * HD :],
    )
    delta = jnp.zeros((1, 2 * rows), jnp.float32)
    for j in range(4):
        at = slice(j * rows, (j + 1) * rows)
        t = lax.dot_general(pieces[j][...], g_ref[...], NT, preferred_element_type=jnp.float32)
        dprob[at] = t
        delta = delta + jnp.sum(prob_ref[at].astype(jnp.float32) * t, axis=0, keepdims=True)
    for j in (2, 3, 0, 1):
        at = slice(j * rows, (j + 1) * rows)
        p = prob_ref[at]
        x = (p.astype(jnp.float32) * (dprob[at] - delta)).astype(jnp.bfloat16)
        dlog_ref[at] = x
        if j >= 2:
            out = slice((j - 2) * rows, (j - 1) * rows)
            dk = jnp.dot(x, q_ref[...], preferred_element_type=jnp.float32)
            dv = jnp.dot(p, g_ref[...], preferred_element_type=jnp.float32)
            send_ref[out, :HD] = (dk * SCALE).astype(jnp.bfloat16)
            send_ref[out, HD:] = dv.astype(jnp.bfloat16)


def terms_kernel(
    index,
    near_ref,
    side_ref,
    rec_ref,
    recs_ref,
    prob_ref,
    q_ref,
    dlog_ref,
    g_ref,
    dq_ref,
    keep_ref,
    k_all,
):
    rows = rec_ref.shape[0]
    own = slice(index * HD, (index + 1) * HD)
    k_all[:rows] = near_ref[:, own]
    k_all[rows : 2 * rows] = rec_ref[:, HD : 2 * HD]
    k_all[2 * rows : 3 * rows] = side_ref[:, own]
    k_all[3 * rows :] = recs_ref[:, HD : 2 * HD]
    for j in range(2):
        at = slice(j * rows, (j + 1) * rows)
        dk = jnp.dot(dlog_ref[at], q_ref[...], preferred_element_type=jnp.float32)
        dv = jnp.dot(prob_ref[at], g_ref[...], preferred_element_type=jnp.float32)
        keep_ref[at, :HD] = dk * SCALE
        keep_ref[at, HD:] = dv
    dq = lax.dot_general(dlog_ref[...], k_all[...], TN, preferred_element_type=jnp.float32)
    dq_ref[...] = (dq * SCALE).astype(jnp.bfloat16)


def vmem_call(kernel, ins, outs, scratch, flops, exps=0, scalars=0):
    vmem, smem = pl.BlockSpec(memory_space=pltpu.VMEM), pl.BlockSpec(memory_space=pltpu.SMEM)
    return pl.pallas_call(
        kernel,
        out_shape=outs,
        in_specs=[smem] * scalars + [vmem] * (len(ins) - scalars),
        out_specs=(vmem,) * len(outs),
        scratch_shapes=scratch,
        compiler_params=pltpu.CompilerParams(vmem_limit_bytes=16 << 20),
        cost_estimate=pl.CostEstimate(
            flops=flops, transcendentals=exps, bytes_accessed=sum(2 * x.size for x in outs)
        ),
    )(*ins)


def prob_call(index, slot_block, reads, q_near, kv_near, kv_side, rec, recs):
    rows = rec.shape[0]
    area = 8 * rows * rows
    return vmem_call(
        functools.partial(prob_kernel, index),
        (slot_block, reads, q_near, kv_near, kv_side, rec, recs),
        (
            jax.ShapeDtypeStruct((4 * rows, 2 * rows), jnp.bfloat16),
            jax.ShapeDtypeStruct((2 * rows, HD), jnp.bfloat16),
        ),
        [pltpu.VMEM((4 * rows, 2 * rows), jnp.float32)],
        2 * area * HD,
        exps=area,
        scalars=2,
    )


def slope_call(hh, index, kv_near, kv_side, rec, recs, grads, prob, q_all):
    rows = rec.shape[0]
    return vmem_call(
        functools.partial(slope_kernel, hh, index),
        (kv_near, kv_side, rec, recs, *grads, prob, q_all),
        (
            jax.ShapeDtypeStruct((4 * rows, 2 * rows), jnp.bfloat16),
            jax.ShapeDtypeStruct((2 * rows, HD), jnp.bfloat16),
            jax.ShapeDtypeStruct((2 * rows, 2 * HD), jnp.bfloat16),
        ),
        [pltpu.VMEM((4 * rows, 2 * rows), jnp.float32)],
        4 * 8 * rows * rows * HD,
    )


def terms_call(index, kv_near, kv_side, rec, recs, prob, q_all, dlog, g_all):
    rows = rec.shape[0]
    return vmem_call(
        functools.partial(terms_kernel, index),
        (kv_near, kv_side, rec, recs, prob, q_all, dlog, g_all),
        (
            jax.ShapeDtypeStruct((2 * rows, HD), jnp.bfloat16),
            jax.ShapeDtypeStruct((2 * rows, 2 * HD), jnp.float32),
        ),
        [pltpu.VMEM((4 * rows, HD), jnp.bfloat16)],
        4 * 8 * rows * rows * HD,
    )


def run_copies(pairs, sems):
    copies = [pltpu.make_async_copy(a, b, sems.at[n]) for n, (a, b) in enumerate(pairs)]
    for copy in copies:
        copy.start()
    for copy in copies:
        copy.wait()


def in_hbm(x):
    return pltpu.with_memory_space_constraint(x, pltpu.HBM)


def copying(kernel, out_shape, count, nbytes, *arrays):
    out_specs = jax.tree.map(lambda _: pl.BlockSpec(memory_space=pltpu.VMEM), out_shape)
    return pl.pallas_call(
        kernel,
        out_shape=out_shape,
        in_specs=[pl.BlockSpec(memory_space=pl.ANY)] * len(arrays),
        out_specs=out_specs,
        scratch_shapes=[pltpu.SemaphoreType.DMA((count,))],
        compiler_params=pltpu.CompilerParams(vmem_limit_bytes=8 << 20),
        cost_estimate=pl.CostEstimate(flops=0, transcendentals=0, bytes_accessed=nbytes),
    )(*arrays)


def pick_gradients(out_grad, nh, half):
    def kernel(g_ref, out_ref, sems):
        far = 1 - lax.axis_index("stretch") // 2
        run_copies(
            [
                (
                    g_ref.at[:, pl.ds(pl.multiple_of((2 * t + far) * half, HD), half)],
                    out_ref.at[:, t * half : (t + 1) * half],
                )
                for t in range(nh)
            ],
            sems,
        )

    shape = jax.ShapeDtypeStruct((out_grad.shape[0], nh * half), out_grad.dtype)
    nbytes = 4 * shape.shape[0] * shape.shape[1]
    return copying(kernel, shape, nh, nbytes, in_hbm(out_grad))


def pick_heads(queries, keys, values, hh):
    rows = queries.shape[0]
    half = hh * HD

    def kernel(q_ref, k_ref, v_ref, *refs):
        outs, q_near, kv_near, sems = refs[:hh], refs[hh], refs[hh + 1], refs[hh + 2]
        side = lax.axis_index("stretch") // 2
        pairs = [
            (
                ref.at[:, pl.ds(pl.multiple_of(((1 - side) * hh + i) * HD, HD), HD)],
                outs[i].at[:, t * HD : (t + 1) * HD],
            )
            for i in range(hh)
            for t, ref in enumerate((q_ref, k_ref, v_ref))
        ]
        stay = pl.ds(pl.multiple_of(side * half, HD), half)
        pairs.append((k_ref.at[:, stay], kv_near.at[:, :half]))
        pairs.append((v_ref.at[:, stay], kv_near.at[:, half:]))
        pairs.append((q_ref.at[:, stay], q_near))
        run_copies(pairs, sems)

    far = jax.ShapeDtypeStruct((rows, 3 * HD), queries.dtype)
    shapes = [far] * hh
    shapes.append(jax.ShapeDtypeStruct((rows, half), queries.dtype))
    shapes.append(jax.ShapeDtypeStruct((rows, 2 * half), queries.dtype))
    nbytes = 12 * rows * 2 * half
    arrays = [in_hbm(x) for x in (queries, keys, values)]
    return copying(kernel, shapes, 3 * hh + 3, nbytes, *arrays)


def pair_gradients(out_grad, g_got, nh, half):
    grad_rows = out_grad.shape[0]

    def kernel(g_ref, got_ref, *refs):
        outs, sems = refs[:-1], refs[-1]
        side, place = lax.axis_index("stretch") // 2, lax.axis_index("head")
        pairs = []
        for d in range(nh):
            target = lax.rem(place + d, nh)
            own = pl.ds(pl.multiple_of((2 * target + side) * half, HD), half)
            got = pl.ds(pl.multiple_of(target * half, HD), half)
            pairs.append((g_ref.at[:, own], outs[d].at[0]))
            pairs.append((got_ref.at[:, got], outs[d].at[1]))
        run_copies(pairs, sems)

    shape = jax.ShapeDtypeStruct((2, grad_rows, half), out_grad.dtype)
    nbytes = 8 * nh * grad_rows * half
    return copying(kernel, [shape] * nh, 2 * nh, nbytes, out_grad, g_got)


def merge_kernel(dq_ref, keep_ref, got_ref, stay_ref, back_ref):
    rows = stay_ref.shape[0]
    total = (keep_ref[...] + got_ref[...].astype(jnp.float32)).astype(jnp.bfloat16)
    stay_ref[:, :HD] = dq_ref[:rows]
    stay_ref[:, HD:] = total[:rows]
    back_ref[:, :HD] = dq_ref[rows:]
    back_ref[:, HD:] = total[rows:]


def merge_call(dq, keep, got):
    rows = dq.shape[0] // 2
    shape = jax.ShapeDtypeStruct((rows, 3 * HD), jnp.bfloat16)
    return pl.pallas_call(
        merge_kernel,
        name="merge_head",
        out_shape=(shape, shape),
        compiler_params=pltpu.CompilerParams(vmem_limit_bytes=8 << 20),
        cost_estimate=pl.CostEstimate(
            flops=rows * HD * 8, transcendentals=0, bytes_accessed=rows * HD * 40
        ),
    )(dq, keep, got)


def finish_kernel(hh, *refs):
    stay, back, outs = refs[:hh], refs[hh : 2 * hh], refs[2 * hh :]
    half = lax.axis_index("stretch") // 2
    for i in range(hh):
        near = pl.ds(pl.multiple_of((half * hh + i) * HD, HD), HD)
        far = pl.ds(pl.multiple_of(((1 - half) * hh + i) * HD, HD), HD)
        for t, out in enumerate(outs):
            out[:, near] = stay[i][:, t * HD : (t + 1) * HD]
            out[:, far] = back[i][:, t * HD : (t + 1) * HD]


def finish_call(stay, back):
    hh = len(stay)
    rows = stay[0].shape[0]
    shape = jax.ShapeDtypeStruct((rows, 2 * hh * HD), jnp.bfloat16)
    vmem = pl.BlockSpec(memory_space=pltpu.VMEM)
    return pl.pallas_call(
        functools.partial(finish_kernel, hh),
        name="finish",
        out_shape=(shape, shape, shape),
        in_specs=[vmem] * (2 * hh),
        out_specs=[vmem] * 3,
        compiler_params=pltpu.CompilerParams(vmem_limit_bytes=12 << 20),
        cost_estimate=pl.CostEstimate(
            flops=0, transcendentals=0, bytes_accessed=rows * HD * hh * 24
        ),
    )(*stay, *back)


def halved(queries, keys, values, out_grad, reads, slot_block):
    _, width = queries.shape
    half = width // 2
    hh = half // HD
    nh = lax.axis_size("head")
    across = lambda x: lax.ppermute(x, "stretch", [(i, i ^ 2) for i in range(4)])
    beside = lambda x: lax.ppermute(x, "stretch", [(i, i ^ 1) for i in range(4)])

    g_far = pick_gradients(out_grad, nh, half)
    g_got = across(g_far)
    *far_heads, q_near, kv_near = pick_heads(queries, keys, values, hh)
    rec, recs = [], []
    for i in range(hh):
        rec.append(across(far_heads[i]))
    kv_side = beside(kv_near)
    for i in range(hh):
        recs.append(beside(rec[i]))

    grads = list(pair_gradients(out_grad, g_got, nh, half))
    for d in range(1, nh):
        grads[d] = lax.ppermute(
            grads[d], "head", [(i, (i + d) % nh) for i in range(nh)]
        )

    stay, back = [], []
    for i in range(hh):
        prob, q_all = prob_call(i, slot_block, reads, q_near, kv_near, kv_side, rec[i], recs[i])
        dlog, g_all, send = slope_call(hh, i, kv_near, kv_side, rec[i], recs[i], grads, prob, q_all)
        dq, keep = terms_call(i, kv_near, kv_side, rec[i], recs[i], prob, q_all, dlog, g_all)
        got = beside(send)
        near, far = merge_call(dq, keep, got)
        back.append(across(far))
        stay.append(near)
    return finish_call(stay, back)


def solution(mesh):
    special = mesh.shape["stretch"] == 4 and mesh.shape["head"] == 4

    def shards(queries, keys, values, out_grad, reads, slot_block):
        heads = queries.shape[1] // HD
        if special and heads == 6:
            return halved(queries, keys, values, out_grad, reads, slot_block)
        return gathered(queries, keys, values, out_grad, reads, slot_block)

    rows = P(("grp", "stretch"), "head")
    return jax.shard_map(
        shards,
        mesh=mesh,
        in_specs=(rows, rows, rows, P(("grp", "stretch", "head"), None), P("grp", None), P("grp")),
        out_specs=(rows, rows, rows),
        check_vma=False,
    )
```

```python
import functools
import math

import jax
import jax.numpy as jnp
from jax import lax
from jax.experimental import pallas as pl
from jax.experimental.pallas import tpu as pltpu
from jax.sharding import PartitionSpec as P

HD = 128
LOG2E = 1.4426950408889634
CLOSED = -1e30
SCALE = 1.0 / math.sqrt(HD)


def pick_rows(table, visit_sequence, index):
    return jnp.sum(jnp.where((visit_sequence == index)[:, None], table, 0), axis=0)


def slopes(q_rows, g_rows, row_logsumexp, row_delta, key_rows, val_rows, mask, scale):
    logits = (
        jnp.einsum("qhd,khd->hqk", q_rows, key_rows, preferred_element_type=jnp.float32) * scale
    )
    prob = jnp.where(mask, jnp.exp(logits - row_logsumexp[:, :, None]), jnp.float32(0.0))
    dprob = jnp.einsum("qhd,khd->hqk", g_rows, val_rows, preferred_element_type=jnp.float32)
    dlogit = (prob * (dprob - row_delta[:, :, None]) * scale).astype(jnp.bfloat16)
    return (prob.astype(jnp.bfloat16), dlogit)


def gathered(queries, keys, values, out_grad, reads, slot_block):
    rows, width = queries.shape
    heads = width // HD
    scale = 1.0 / math.sqrt(HD)
    grads_in = lax.all_to_all(out_grad, "head", split_axis=1, concat_axis=0, tiled=True)
    slot_count = lax.axis_size("stretch")
    slot = lax.axis_index("stretch")
    visit_sequence = jnp.arange(slot_count, dtype=jnp.int32)
    mine = jnp.sum(jnp.where(visit_sequence == slot, slot_block, 0))
    same_table = slot_block[:, None] == visit_sequence[None, :]
    read_row = pick_rows(reads, visit_sequence, mine)
    own_reads = jnp.sum(jnp.where(same_table, read_row[None, :], 0), axis=1)
    key_open = (slot_block == mine) | (slot_block < mine) & (own_reads == 1)
    q_three = queries.reshape(rows, heads, HD)
    g_three = grads_in.reshape(rows, heads, HD)
    key_whole, val_whole = (
        lax.all_gather(keys, "stretch", axis=0, tiled=True),
        lax.all_gather(values, "stretch", axis=0, tiled=True),
    )
    total = key_whole.shape[0]
    per_iteration = -(-512 // rows)
    while slot_count % per_iteration:
        per_iteration -= 1
    span = rows * per_iteration
    nspan = total // span
    key_mask = jnp.repeat(key_open, rows)
    key_blocks = key_whole.reshape(nspan, span, heads, HD)
    val_blocks = val_whole.reshape(nspan, span, heads, HD)
    mask_blocks = key_mask.reshape(nspan, span)

    def forward_step(carry, block):
        top, mass, accum = carry
        key_block_tile, value_block_tile, open_blk = block
        logits = (
            jnp.einsum("qhd,khd->hqk", q_three, key_block_tile, preferred_element_type=jnp.float32)
            * scale
        )
        masked_logits = jnp.where(open_blk[None, None, :], logits, jnp.float32(-1e30))
        new_top = jnp.maximum(top, jnp.max(masked_logits, axis=-1))
        weights = jnp.where(
            open_blk[None, None, :], jnp.exp(masked_logits - new_top[:, :, None]), jnp.float32(0.0)
        )
        shrink = jnp.exp(top - new_top)
        mass = mass * shrink + jnp.sum(weights, axis=-1)
        accum = accum * shrink[:, :, None] + jnp.einsum(
            "hqk,khd->hqd",
            weights.astype(jnp.bfloat16),
            value_block_tile,
            preferred_element_type=jnp.float32,
        )
        return ((new_top, mass, accum), None)

    start_top = jnp.full((heads, rows), -1e30, jnp.float32)
    start_mass = jnp.zeros((heads, rows), jnp.float32)
    start_accum = jnp.zeros((heads, rows, HD), jnp.float32)
    (top, mass, accum), _ = lax.scan(
        forward_step, (start_top, start_mass, start_accum), (key_blocks, val_blocks, mask_blocks)
    )
    row_logsumexp = top + jnp.log(mass)
    attended = (accum / mass[:, :, None]).astype(jnp.bfloat16)
    row_delta = jnp.einsum("qhd,hqd->hq", g_three, attended, preferred_element_type=jnp.float32)
    dquery_start = jnp.zeros((rows, heads, HD), jnp.float32)

    def joined_step(dquery, block):
        key_block_tile, value_block_tile, open_blk = block
        prob_low, dlogit = slopes(
            q_three,
            g_three,
            row_logsumexp,
            row_delta,
            key_block_tile,
            value_block_tile,
            open_blk[None, None, :],
            scale,
        )
        dquery = dquery + jnp.einsum(
            "hqk,khd->qhd", dlogit, key_block_tile, preferred_element_type=jnp.float32
        )
        dkey = jnp.einsum("hqk,qhd->khd", dlogit, q_three, preferred_element_type=jnp.float32)
        dval = jnp.einsum("hqk,qhd->khd", prob_low, g_three, preferred_element_type=jnp.float32)
        terms = jnp.concatenate([dkey.reshape(span, width), dval.reshape(span, width)], axis=1)
        return (dquery, terms)

    dquery, stacked = lax.scan(joined_step, dquery_start, (key_blocks, val_blocks, mask_blocks))
    query_grad = dquery.reshape(rows, width).astype(jnp.bfloat16)
    both = lax.psum_scatter(
        stacked.reshape(total, 2 * width).astype(jnp.bfloat16),
        "stretch",
        scatter_dimension=0,
        tiled=True,
    ).astype(jnp.float32)
    key_grad = both[:, :width].astype(jnp.bfloat16)
    value_grad = both[:, width:].astype(jnp.bfloat16)
    return (query_grad, key_grad, value_grad)


NT = (((1,), (1,)), ((), ()))


def shift_kernel(block_ref, reads_ref, shift_ref):
    rows = shift_ref.shape[1] // 2
    slot = lax.axis_index("stretch")
    block, reads = block_ref[...], reads_ref[...]
    one = lax.broadcasted_iota(jnp.int32, block.shape, 1)
    down = lax.broadcasted_iota(jnp.int32, reads.shape, 0)
    along = lax.broadcasted_iota(jnp.int32, reads.shape, 1)
    lane = lax.broadcasted_iota(jnp.int32, (1, 2 * rows), 1)

    def total(x):
        return jnp.sum(jnp.sum(x, axis=1, keepdims=True), axis=0, keepdims=True)

    held = [total(jnp.where(one == (slot ^ j), block, 0)) for j in range(4)]

    def shut(first, second):
        linked = total(jnp.where((down == first) & (along == second), reads, 0))
        seen = (first == second) | ((second < first) & (linked == 1))
        return jnp.where(seen, jnp.float32(0.0), jnp.float32(CLOSED))

    for j, k in enumerate((0, 2, 1, 3)):
        near, far = shut(held[0], held[k]), shut(held[2], held[k])
        shift_ref[j : j + 1] = jnp.where(lane < rows, near, far)


def prob_kernel(
    index,
    shift_ref,
    q_ref,
    near_ref,
    side_ref,
    rec_ref,
    recs_ref,
    weight_ref,
    q_all,
    inv_ref,
    inv_row_ref,
    score,
):
    rows = q_ref.shape[0]
    own = slice(index * HD, (index + 1) * HD)
    q_all[:rows] = q_ref[:, own]
    q_all[rows:] = rec_ref[:, :HD]
    pieces = (
        near_ref.at[:, own],
        rec_ref.at[:, HD : 2 * HD],
        side_ref.at[:, own],
        recs_ref.at[:, HD : 2 * HD],
    )
    shifts, tops = [], []
    for j, piece in enumerate(pieces):
        s = lax.dot_general(piece[...], q_all[...], NT, preferred_element_type=jnp.float32)
        score[j * rows : (j + 1) * rows] = s
        shifts.append(shift_ref[j : j + 1])
        tops.append(jnp.max(s, axis=0, keepdims=True) * (LOG2E * SCALE) + shifts[j])
    top = jnp.maximum(jnp.maximum(tops[0], tops[1]), jnp.maximum(tops[2], tops[3]))
    mass = jnp.zeros((1, 2 * rows), jnp.float32)
    for j in range(4):
        at = slice(j * rows, (j + 1) * rows)
        e = jnp.exp2(score[at] * (LOG2E * SCALE) - (top - shifts[j]))
        weight_ref[at] = e.astype(jnp.bfloat16)
        mass = mass + jnp.sum(e, axis=0, keepdims=True)
    inv = 1.0 / mass
    inv_row_ref[...] = jnp.broadcast_to(inv, (8, 2 * rows))
    inv_ref[...] = jnp.broadcast_to(inv, (HD, 2 * rows)).T


def slope_kernel(
    hh,
    index,
    near_ref,
    side_ref,
    rec_ref,
    recs_ref,
    *refs,
):
    weight_ref, q_ref, inv_ref, inv_row_ref, dlog_ref, g_ref, send_ref, dprob = refs[-8:]
    rows = rec_ref.shape[0]
    grad_rows = refs[0].shape[0]
    place = lax.axis_index("head")
    nh = rows // grad_rows
    own = slice((hh + index) * HD, (hh + index + 1) * HD)
    for d in range(nh):
        base = lax.rem(place - d + nh, nh) * grad_rows
        for i in range(2):
            at = pl.multiple_of(base + i * rows, 16)
            part = refs[i * nh + d][:, index * HD : (index + 1) * HD].astype(jnp.float32)
            part = part * inv_ref[pl.ds(at, grad_rows), :]
            g_ref[pl.ds(at, grad_rows), :] = part.astype(jnp.bfloat16)
    pieces = (
        near_ref.at[:, own],
        rec_ref.at[:, 2 * HD :],
        side_ref.at[:, own],
        recs_ref.at[:, 2 * HD :],
    )
    delta = jnp.zeros((1, 2 * rows), jnp.float32)
    for j in range(4):
        at = slice(j * rows, (j + 1) * rows)
        t = lax.dot_general(pieces[j][...], g_ref[...], NT, preferred_element_type=jnp.float32)
        dprob[at] = t
        delta = delta + jnp.sum(weight_ref[at].astype(jnp.float32) * t, axis=0, keepdims=True)
    delta = delta * inv_row_ref[0:1]

    def value_term(j):
        at = slice(j * rows, (j + 1) * rows)
        dv = jnp.dot(weight_ref[at], g_ref[...], preferred_element_type=jnp.float32)
        send_ref[(j - 2) * rows : (j - 1) * rows, HD:] = dv.astype(jnp.bfloat16)

    def key_term(j):
        at = slice(j * rows, (j + 1) * rows)
        dk = jnp.dot(dlog_ref[at], q_ref[...], preferred_element_type=jnp.float32)
        send_ref[(j - 2) * rows : (j - 1) * rows, :HD] = (dk * SCALE).astype(jnp.bfloat16)

    def slope(j):
        at = slice(j * rows, (j + 1) * rows)
        x = weight_ref[at].astype(jnp.float32) * (dprob[at] - delta)
        dlog_ref[at] = x.astype(jnp.bfloat16)

    value_term(2)
    slope(2)
    value_term(3)
    slope(3)
    key_term(2)
    slope(0)
    key_term(3)
    slope(1)


def terms_kernel(
    index,
    near_ref,
    side_ref,
    rec_ref,
    recs_ref,
    weight_ref,
    g_ref,
    q_ref,
    dlog_ref,
    dq_ref,
    keep_ref,
    k_all,
):
    rows = rec_ref.shape[0]
    own = slice(index * HD, (index + 1) * HD)
    k_all[:rows] = near_ref[:, own]
    k_all[rows : 2 * rows] = rec_ref[:, HD : 2 * HD]
    k_all[2 * rows : 3 * rows] = side_ref[:, own]
    k_all[3 * rows :] = recs_ref[:, HD : 2 * HD]
    for j in range(2):
        at = slice(j * rows, (j + 1) * rows)
        dk = jnp.dot(dlog_ref[at], q_ref[...], preferred_element_type=jnp.float32)
        keep_ref[at, :HD] = dk * SCALE
        dv = jnp.dot(weight_ref[at], g_ref[...], preferred_element_type=jnp.float32)
        keep_ref[at, HD:] = dv
    dq = jnp.dot(k_all[...].T, dlog_ref[...], preferred_element_type=jnp.float32).T
    dq_ref[...] = (dq * SCALE).astype(jnp.bfloat16)


def vmem_call(kernel, ins, outs, scratch, flops, exps=0):
    vmem = pl.BlockSpec(memory_space=pltpu.VMEM)
    return pl.pallas_call(
        kernel,
        out_shape=outs,
        in_specs=[vmem] * len(ins),
        out_specs=(vmem,) * len(outs),
        scratch_shapes=scratch,
        compiler_params=pltpu.CompilerParams(vmem_limit_bytes=16 << 20),
        cost_estimate=pl.CostEstimate(
            flops=flops, transcendentals=exps, bytes_accessed=sum(2 * x.size for x in outs)
        ),
    )(*ins)


def prob_call(index, shift, q_near, kv_near, kv_side, rec, recs):
    rows = rec.shape[0]
    area = 8 * rows * rows
    return vmem_call(
        functools.partial(prob_kernel, index),
        (shift, q_near, kv_near, kv_side, rec, recs),
        (
            jax.ShapeDtypeStruct((4 * rows, 2 * rows), jnp.bfloat16),
            jax.ShapeDtypeStruct((2 * rows, HD), jnp.bfloat16),
            jax.ShapeDtypeStruct((2 * rows, HD), jnp.float32),
            jax.ShapeDtypeStruct((8, 2 * rows), jnp.float32),
        ),
        [pltpu.VMEM((4 * rows, 2 * rows), jnp.float32)],
        2 * area * HD,
        exps=area,
    )


def slope_call(hh, index, kv_near, kv_side, rec, recs, grads, weight, q_all, inv, inv_row):
    rows = rec.shape[0]
    return vmem_call(
        functools.partial(slope_kernel, hh, index),
        (kv_near, kv_side, rec, recs, *grads, weight, q_all, inv, inv_row),
        (
            jax.ShapeDtypeStruct((4 * rows, 2 * rows), jnp.bfloat16),
            jax.ShapeDtypeStruct((2 * rows, HD), jnp.bfloat16),
            jax.ShapeDtypeStruct((2 * rows, 2 * HD), jnp.bfloat16),
        ),
        [pltpu.VMEM((4 * rows, 2 * rows), jnp.float32)],
        4 * 8 * rows * rows * HD,
    )


def terms_call(index, kv_near, kv_side, rec, recs, weight, g_all, q_all, dlog):
    rows = rec.shape[0]
    return vmem_call(
        functools.partial(terms_kernel, index),
        (kv_near, kv_side, rec, recs, weight, g_all, q_all, dlog),
        (
            jax.ShapeDtypeStruct((2 * rows, HD), jnp.bfloat16),
            jax.ShapeDtypeStruct((2 * rows, 2 * HD), jnp.float32),
        ),
        [pltpu.VMEM((4 * rows, HD), jnp.bfloat16)],
        4 * 8 * rows * rows * HD,
    )


def run_copies(pairs, sems):
    copies = [pltpu.make_async_copy(a, b, sems.at[n]) for n, (a, b) in enumerate(pairs)]
    for copy in copies:
        copy.start()
    for copy in copies:
        copy.wait()


def in_hbm(x):
    return pltpu.with_memory_space_constraint(x, pltpu.HBM)


def copying(kernel, out_shape, count, nbytes, *arrays):
    out_specs = jax.tree.map(lambda _: pl.BlockSpec(memory_space=pltpu.VMEM), out_shape)
    return pl.pallas_call(
        kernel,
        out_shape=out_shape,
        in_specs=[pl.BlockSpec(memory_space=pl.ANY)] * len(arrays),
        out_specs=out_specs,
        scratch_shapes=[pltpu.SemaphoreType.DMA((count,))],
        compiler_params=pltpu.CompilerParams(vmem_limit_bytes=8 << 20),
        cost_estimate=pl.CostEstimate(flops=0, transcendentals=0, bytes_accessed=nbytes),
    )(*arrays)


def pick_gradients(out_grad, nh, half):
    def kernel(g_ref, out_ref, sems):
        far = 1 - lax.axis_index("stretch") // 2
        run_copies(
            [
                (
                    g_ref.at[:, pl.ds(pl.multiple_of((2 * t + far) * half, HD), half)],
                    out_ref.at[:, t * half : (t + 1) * half],
                )
                for t in range(nh)
            ],
            sems,
        )

    shape = jax.ShapeDtypeStruct((out_grad.shape[0], nh * half), out_grad.dtype)
    nbytes = 4 * shape.shape[0] * shape.shape[1]
    return copying(kernel, shape, nh, nbytes, in_hbm(out_grad))


def pick_heads(queries, keys, values, out_grad, hh, nh):
    rows = queries.shape[0]
    half = hh * HD

    def kernel(q_ref, k_ref, v_ref, g_ref, *refs):
        outs, q_near, kv_near, grads = refs[:hh], refs[hh], refs[hh + 1], refs[hh + 2 : -1]
        sems, place = refs[-1], lax.axis_index("head")
        side = lax.axis_index("stretch") // 2
        pairs = [
            (
                ref.at[:, pl.ds(pl.multiple_of(((1 - side) * hh + i) * HD, HD), HD)],
                outs[i].at[:, t * HD : (t + 1) * HD],
            )
            for i in range(hh)
            for t, ref in enumerate((q_ref, k_ref, v_ref))
        ]
        stay = pl.ds(pl.multiple_of(side * half, HD), half)
        pairs.append((k_ref.at[:, stay], kv_near.at[:, :half]))
        pairs.append((v_ref.at[:, stay], kv_near.at[:, half:]))
        pairs.append((q_ref.at[:, stay], q_near))
        for d in range(nh):
            group = lax.rem(place + d, nh) * 2 + side
            pairs.append((g_ref.at[:, pl.ds(pl.multiple_of(group * half, HD), half)], grads[d]))
        run_copies(pairs, sems)

    far = jax.ShapeDtypeStruct((rows, 3 * HD), queries.dtype)
    shapes = [far] * hh
    shapes.append(jax.ShapeDtypeStruct((rows, half), queries.dtype))
    shapes.append(jax.ShapeDtypeStruct((rows, 2 * half), queries.dtype))
    shapes += [jax.ShapeDtypeStruct((out_grad.shape[0], half), queries.dtype)] * nh
    nbytes = 14 * rows * 2 * half
    arrays = [in_hbm(x) for x in (queries, keys, values, out_grad)]
    return copying(kernel, shapes, 3 * hh + 3 + nh, nbytes, *arrays)


def split_gradients(g_got, nh, half):
    def kernel(got_ref, *refs):
        place = lax.axis_index("head")
        pairs = []
        for d in range(nh):
            at = pl.multiple_of(lax.rem(place + d, nh) * half, HD)
            pairs.append((got_ref.at[:, pl.ds(at, half)], refs[d]))
        run_copies(pairs, refs[-1])

    shape = jax.ShapeDtypeStruct((g_got.shape[0], half), g_got.dtype)
    nbytes = 4 * g_got.size
    return copying(kernel, [shape] * nh, nh, nbytes, g_got)


def merge_kernel(dq_ref, keep_ref, got_ref, stay_ref, back_ref):
    rows = stay_ref.shape[0]
    total = (keep_ref[...] + got_ref[...].astype(jnp.float32)).astype(jnp.bfloat16)
    stay_ref[:, :HD] = dq_ref[:rows]
    stay_ref[:, HD:] = total[:rows]
    back_ref[:, :HD] = dq_ref[rows:]
    back_ref[:, HD:] = total[rows:]


def merge_call(dq, keep, got):
    rows = dq.shape[0] // 2
    shape = jax.ShapeDtypeStruct((rows, 3 * HD), jnp.bfloat16)
    return pl.pallas_call(
        merge_kernel,
        name="merge_head",
        out_shape=(shape, shape),
        compiler_params=pltpu.CompilerParams(vmem_limit_bytes=8 << 20),
        cost_estimate=pl.CostEstimate(
            flops=rows * HD * 8, transcendentals=0, bytes_accessed=rows * HD * 40
        ),
    )(dq, keep, got)


def place_call(hh, parts, outs):
    rows = parts[0][0].shape[0]
    count = len(parts)

    def kernel(*refs):
        outs, sems = refs[-4:-1], refs[-1]
        side = lax.axis_index("stretch") // 2
        pairs = []
        for ref, (_, i, far) in zip(refs, parts):
            half = 1 - side if far else side
            to = pl.ds(pl.multiple_of((half * hh + i) * HD, HD), HD)
            for t, out in enumerate(outs):
                pairs.append((ref.at[:, t * HD : (t + 1) * HD], out.at[:, to]))
        run_copies(pairs, sems)

    given = list(outs) if outs else []
    shape = jax.ShapeDtypeStruct((rows, 2 * hh * HD), jnp.bfloat16)
    return pl.pallas_call(
        kernel,
        out_shape=(shape,) * 3,
        in_specs=[pl.BlockSpec(memory_space=pltpu.VMEM)] * count
        + [pl.BlockSpec(memory_space=pl.ANY)] * len(given),
        out_specs=(pl.BlockSpec(memory_space=pltpu.HBM),) * 3,
        scratch_shapes=[pltpu.SemaphoreType.DMA((3 * count,))],
        input_output_aliases={count + t: t for t in range(len(given))},
        compiler_params=pltpu.CompilerParams(vmem_limit_bytes=4 << 20),
        cost_estimate=pl.CostEstimate(
            flops=0, transcendentals=0, bytes_accessed=count * rows * HD * 12
        ),
    )(*(part for part, _, _ in parts), *given)


def halved(queries, keys, values, out_grad, reads, slot_block):
    rows, width = queries.shape
    half = width // 2
    hh = half // HD
    nh = lax.axis_size("head")
    across = lambda x: lax.ppermute(x, "stretch", [(i, i ^ 2) for i in range(4)])
    beside = lambda x: lax.ppermute(x, "stretch", [(i, i ^ 1) for i in range(4)])

    g_far = pick_gradients(out_grad, nh, half)
    g_got = across(g_far)
    picked = pick_heads(queries, keys, values, out_grad, hh, nh)
    far_heads, q_near, kv_near = picked[:hh], picked[hh], picked[hh + 1]
    mine = list(picked[hh + 2 :])
    shape = jax.ShapeDtypeStruct((4, 2 * rows), jnp.float32)
    (shift,) = vmem_call(shift_kernel, (slot_block.reshape(1, -1), reads), (shape,), [], 0)
    rec, recs = [], []
    for i in range(hh):
        rec.append(across(far_heads[i]))
    kv_side = beside(kv_near)
    for i in range(hh):
        recs.append(beside(rec[i]))

    def onward(x, d):
        return lax.ppermute(x, "head", [(i, (i + d) % nh) for i in range(nh)])

    for d in range(1, nh):
        mine[d] = onward(mine[d], d)
    theirs = list(split_gradients(g_got, nh, half))
    for d in range(1, nh):
        theirs[d] = onward(theirs[d], d)
    grads = mine + theirs

    stay, back = [], []
    for i in range(hh):
        weight, q_all, inv, inv_row = prob_call(i, shift, q_near, kv_near, kv_side, rec[i], recs[i])
        dlog, g_all, send = slope_call(
            hh, i, kv_near, kv_side, rec[i], recs[i], grads, weight, q_all, inv, inv_row
        )
        dq, keep = terms_call(i, kv_near, kv_side, rec[i], recs[i], weight, g_all, q_all, dlog)
        got = beside(send)
        near, far = merge_call(dq, keep, got)
        back.append(across(far))
        stay.append(near)
    parts = [(x, i, False) for i, x in enumerate(stay)]
    parts += [(x, i, True) for i, x in enumerate(back)]
    outs = place_call(hh, parts[:-1], None)
    return place_call(hh, parts[-1:], outs)


def solution(mesh):
    special = mesh.shape["stretch"] == 4 and mesh.shape["head"] == 4

    def shards(queries, keys, values, out_grad, reads, slot_block):
        heads = queries.shape[1] // HD
        if special and heads == 6:
            return halved(queries, keys, values, out_grad, reads, slot_block)
        return gathered(queries, keys, values, out_grad, reads, slot_block)

    rows = P(("grp", "stretch"), "head")
    return jax.shard_map(
        shards,
        mesh=mesh,
        in_specs=(rows, rows, rows, P(("grp", "stretch", "head"), None), P("grp", None), P("grp")),
        out_specs=(rows, rows, rows),
        check_vma=False,
    )
```
